32 devices in a mesh: groups: 2 (over y), blk: 4 (over x, core), ulysses: 4 (over z).
Axes of the slice: x: 2, y: 2, z: 4, core: 2. Of those that a mesh axis runs over, the one named last changes fastest.
Arguments:
- query_proj: bfloat16 [1024, 1024], P(('groups', 'blk', 'ulysses')), parts along dimension 0, may hold values from -200 to 200
- key_proj: bfloat16 [1024, 1024], P(('groups', 'blk', 'ulysses')), parts along dimension 0, may hold values from -200 to 200
- value_proj: bfloat16 [1024, 1024], P(('groups', 'blk', 'ulysses')), parts along dimension 0, may hold values from -6 to 6
- query_gain: float32 [1024], replicated, may hold values from 1.2 to 2.4
- key_gain: float32 [1024], replicated, may hold values from 1.2 to 2.4
- control: bfloat16 [1024, 384], P(('groups', 'blk', 'ulysses')), parts along dimension 0, may hold values from -6 to 6
- hint_weight: bfloat16 [384, 1024], replicated, may hold values from -0.3125 to 0.3125
- hint_gain: float32 [8, 1024], replicated, may hold values from 0.3 to 3
- owner_map: int32 [32, 4], P(('groups', 'blk', 'ulysses')), parts along dimension 0, may hold values from 0 to 3, each once within a row
- layer_index: int32 [32], P(('groups', 'blk', 'ulysses')), parts along dimension 0, may hold values from 0 to 7
Outputs:
- block_out: bfloat16 [1024, 1024], P(('groups', 'blk', 'ulysses')), parts along dimension 0
The draws below stay inside these ranges and needn't reach their ends.
There are 2 independent parts, one for each index of `groups`. The reference program is written for one: setup_inputs(seed, part) draws one part's arguments, and reference() takes and returns one part's arrays. A program takes and returns all parts, laid end to end along the dimension named above; an argument that names none is the same for every part. Nothing has to cross between parts.
Inputs may be any that keep to these rules, and one draw needn't show every extreme that they name: `owner_map`: each row is a permutation of 0 to 3.
All inputs are finite; a program needn't handle non-finite values.
Results may differ from the reference program's by a relative error of at most 0.008.
Values may be sent and summed in bfloat16 or wider, within the bound.
A program may use at most 64 MiB of HBM per device.

```python
import math
import jax
import jax.numpy as jnp
from jax import lax

HEAD_DIM = 128
HEADS = 8
FEATS = 1024
CTRL_IN = 384
CTRL_LAYERS = 8
TOK_DEV = 32
SLAB = 8
TOKENS = 512
N_BLK = 4
N_ULYSSES = 4


def paired_draw(key):
    base_q = jax.random.fold_in(key, 11)
    base_k = jax.random.fold_in(key, 12)
    column_key = jax.random.fold_in(key, 13)
    columns = jnp.exp(jax.random.uniform(column_key, (FEATS,), jnp.float32, 0.0, 2.302585))
    query_rows = jax.random.truncated_normal(base_q, -4.0, 4.0, (TOKENS, FEATS), jnp.float32) * columns
    key_rows = jax.random.truncated_normal(base_k, -4.0, 4.0, (TOKENS, FEATS), jnp.float32) * columns
    query_rows = jnp.clip(query_rows, -200.0, 200.0)
    key_rows = jnp.clip(key_rows, -200.0, 200.0)
    return (query_rows, key_rows)


def draw_query_proj(key, part):
    return paired_draw(key)[0].astype(jnp.bfloat16)


def draw_key_proj(key, part):
    return paired_draw(key)[1].astype(jnp.bfloat16)


def set_ends(entries, key, smallest, high):
    shape = entries.shape
    place = [jax.random.randint(jax.random.fold_in(key, axis), (), 0, shape[axis]) for axis in range(len(shape))]
    entries = entries.at[tuple(place)].set(smallest)
    longest = shape.index(max(shape))
    place[longest] = (place[longest] + 1) % shape[longest]
    return entries.at[tuple(place)].set(high)


def block_levels(key, extent, cuts, low, top_value):
    level = 1.0
    for axis_at, blocks in cuts:
        steps = jax.random.uniform(jax.random.fold_in(jax.random.fold_in(key, 6), axis_at), (blocks,), jnp.float32, low / len(cuts), top_value / len(cuts))
        level = level * jnp.repeat(jnp.exp(steps), extent[axis_at] // blocks).reshape((-1,) + (1,) * (len(extent) - 1 - axis_at))
    return level


def normal_values(own_key, dims, deviation, most, shards=(), held_as=jnp.bfloat16):
    level = block_levels(own_key, dims, shards, -0.22, 0.18) if shards else 1.0
    values = jax.random.normal(own_key, dims, jnp.float32) * deviation * level
    return jnp.minimum(jnp.maximum(values, -most), most).astype(held_as)


def setup_inputs(seed: int = 0, part: int = 0) -> dict:
    key_list = jax.random.split(jax.random.key(seed), 11)
    own_keys = jax.random.split(jax.random.fold_in(key_list[10], part), 11)
    query_proj = draw_query_proj(jax.random.fold_in(jax.random.fold_in(key_list[10], part), 71), part)
    key_proj = draw_key_proj(jax.random.fold_in(jax.random.fold_in(key_list[10], part), 71), part)
    value_proj = normal_values(own_keys[2], (TOKENS, FEATS), 1.0, 6.0, ((0, 16),))
    query_gain = jnp.clip(jax.random.uniform(key_list[3], (FEATS,), jnp.float32, 1.2, 2.4), 1.2, 2.4)
    key_gain = jnp.clip(jax.random.uniform(key_list[4], (FEATS,), jnp.float32, 1.2, 2.4), 1.2, 2.4)
    control = normal_values(own_keys[5], (TOKENS, CTRL_IN), 1.0, 6.0, ((0, 16),))
    hint_weight = normal_values(key_list[6], (CTRL_IN, FEATS), CTRL_IN ** -0.5, 0.3125)
    hint_gain = jnp.clip(jnp.exp(jax.random.uniform(key_list[7], (CTRL_LAYERS, FEATS), jnp.float32, math.log(0.3), math.log(3.0))), 0.3, 3.0)
    owner_map = jax.vmap(lambda own: jax.random.permutation(own, N_ULYSSES))(jax.random.split(own_keys[8], (N_BLK * N_ULYSSES))).reshape((N_BLK * N_ULYSSES, N_ULYSSES)).astype(jnp.int32)
    layer_index = set_ends(jax.random.randint(own_keys[9], (N_BLK * N_ULYSSES,), 0, CTRL_LAYERS), jax.random.fold_in(own_keys[9], 1), 0, CTRL_LAYERS - 1).astype(jnp.int32)
    return dict(query_proj=query_proj, key_proj=key_proj, value_proj=value_proj, query_gain=query_gain, key_gain=key_gain, control=control, hint_weight=hint_weight, hint_gain=hint_gain, owner_map=owner_map, layer_index=layer_index)


def normalize_rows(rows, gain):
    values = rows.astype(jnp.float32)
    scale = lax.rsqrt(lax.optimization_barrier(jnp.mean(values * values, axis=-1, keepdims=True)) + 1e-06)
    return (values * scale * gain).astype(jnp.bfloat16)

def query_block_size(count):
    block = min(count, 1024)
    while count % block:
        block = block - 1
    return block

def one_head(triple):
    queries, keys, values = triple
    count = queries.shape[0]
    block = query_block_size(count)
    shaped = queries.reshape(count // block, block, HEAD_DIM)

    def per_block(query_rows):
        scores = jnp.dot(query_rows, keys.T, preferred_element_type=jnp.float32) * HEAD_DIM ** (-0.5)
        peak = lax.optimization_barrier(jnp.max(scores, axis=-1, keepdims=True))
        expo = jnp.exp(scores - peak)
        totals = lax.optimization_barrier(jnp.sum(expo, axis=-1, keepdims=True))
        probs = expo.astype(jnp.bfloat16)
        mixed = jnp.dot(probs, values, preferred_element_type=jnp.float32)
        return (mixed / totals).astype(jnp.bfloat16)
    return lax.map(per_block, shaped).reshape(count, HEAD_DIM)

def reference(query_proj, key_proj, value_proj, query_gain, key_gain, control, hint_weight, hint_gain, owner_map, layer_index):
    count = query_proj.shape[0]
    query_normed = normalize_rows(query_proj, query_gain)
    key_normed = normalize_rows(key_proj, key_gain)
    split_q = query_normed.reshape(count, HEADS, HEAD_DIM).transpose(1, 0, 2)
    split_k = key_normed.reshape(count, HEADS, HEAD_DIM).transpose(1, 0, 2)
    split_v = value_proj.reshape(count, HEADS, HEAD_DIM).transpose(1, 0, 2)
    attended = lax.map(one_head, (split_q, split_k, split_v))
    attended = attended.transpose(1, 0, 2).reshape(count, FEATS)
    control_normed = normalize_rows(control, jnp.float32(1.0))
    hint = jnp.dot(control_normed, hint_weight, preferred_element_type=jnp.float32).astype(jnp.bfloat16)
    slabs = hint.reshape(N_BLK, N_ULYSSES, N_ULYSSES, SLAB, FEATS)
    owners = owner_map.reshape(N_BLK, N_ULYSSES, N_ULYSSES)
    positions = jnp.arange(N_ULYSSES, dtype=jnp.int32)
    match = (owners[:, :, :, None] == positions[None, None, None, :]).astype(jnp.int32)
    inverse = lax.optimization_barrier(jnp.sum(positions[None, None, :, None] * match, axis=2)).astype(jnp.int32)
    picked = jnp.take_along_axis(slabs, inverse[:, :, :, None, None], axis=2)
    placed = picked.transpose(0, 2, 1, 3, 4).reshape(N_BLK * N_ULYSSES, TOK_DEV, FEATS)
    gains = jnp.take(hint_gain, layer_index.astype(jnp.int32), axis=0)
    scaled = (placed.astype(jnp.float32) * gains[:, None, :]).reshape(count, FEATS)
    return (attended.astype(jnp.float32) + scaled).astype(jnp.bfloat16)
```

```python
import functools
import math

import jax
import jax.numpy as jnp
from jax import lax
from jax.experimental import pallas as pl
from jax.experimental.pallas import tpu as pltpu
from jax.sharding import PartitionSpec as P

HEAD_DIM = 128
CORES = 2
MESH = pl.DeviceIdType.MESH


def normalize_rows(rows, gain):
    values = rows.astype(jnp.float32)
    scale = lax.rsqrt(jnp.mean(values * values, axis=-1, keepdims=True) + 1e-06)
    return (values * scale * gain).astype(jnp.bfloat16)


def block_size(count):
    block = min(count, 1024)
    while count % block:
        block = block - 1
    return block


def make_fold(queries):
    rows = queries.shape[0]
    heads = queries.shape[1] // HEAD_DIM
    shaped = queries.reshape(rows, heads, HEAD_DIM)
    factor = HEAD_DIM ** (-0.5)

    def update(state, pair):
        peak, totals, accum = state
        key_block, value_block = pair
        scores = (
            jnp.einsum("qhd,khd->hqk", shaped, key_block, preferred_element_type=jnp.float32)
            * factor
        )
        new_peak = jnp.maximum(peak, jnp.max(scores, axis=-1))
        correction = jnp.exp(peak - new_peak)
        expo = jnp.exp(scores - new_peak[:, :, None])
        totals = totals * correction + jnp.sum(expo, axis=-1)
        mixed = jnp.einsum(
            "hqk,khd->hqd",
            expo.astype(jnp.bfloat16),
            value_block,
            preferred_element_type=jnp.float32,
        )
        accum = accum * correction[:, :, None] + mixed
        return ((new_peak, totals, accum), None)

    def fold(carry, piece, start):
        keys, values = piece
        count = keys.shape[0]
        block = block_size(count)
        key_blocks = keys.reshape(count // block, block, heads, HEAD_DIM)
        value_blocks = values.reshape(count // block, block, heads, HEAD_DIM)
        result, unused = lax.scan(update, carry, (key_blocks, value_blocks))
        return result

    start_state = (
        jnp.full((heads, rows), -1e30, jnp.float32),
        jnp.zeros((heads, rows), jnp.float32),
        jnp.zeros((heads, rows, HEAD_DIM), jnp.float32),
    )
    return (fold, start_state)


def finish(state):
    peak, totals, accum = state
    heads, rows = totals.shape
    output = (accum / totals[:, :, None]).astype(jnp.bfloat16)
    return output.transpose(1, 0, 2).reshape(rows, heads * HEAD_DIM)


def make_hint(patches, hint_weight):
    normed = normalize_rows(patches, jnp.float32(1.0))
    return jnp.dot(normed, hint_weight, preferred_element_type=jnp.float32).astype(jnp.bfloat16)


def shards(
    query_proj,
    key_proj,
    value_proj,
    query_gain,
    key_gain,
    control,
    hint_weight,
    hint_gain,
    owner_map,
    layer_index,
):
    query_normed = normalize_rows(query_proj, query_gain)
    key_normed = normalize_rows(key_proj, key_gain)
    query_heads, key_heads, value_heads = (
        lax.all_to_all(query_normed, "ulysses", split_axis=1, concat_axis=0, tiled=True),
        lax.all_to_all(key_normed, "ulysses", split_axis=1, concat_axis=0, tiled=True),
        lax.all_to_all(value_proj, "ulysses", split_axis=1, concat_axis=0, tiled=True),
    )
    fold, start_state = make_fold(query_heads)
    state = fold(
        start_state,
        (
            lax.all_gather(key_heads, "blk", axis=0, tiled=True),
            lax.all_gather(value_heads, "blk", axis=0, tiled=True),
        ),
        jnp.int32(0),
    )
    attended = lax.all_to_all(finish(state), "ulysses", split_axis=0, concat_axis=1, tiled=True)
    owners = lax.axis_size("ulysses")
    tok_rows = control.shape[0]
    slab_rows = tok_rows // owners
    positions = jnp.arange(owners, dtype=jnp.int32)
    match = (owner_map[0][:, None] == positions[None, :]).astype(jnp.int32)
    inverse = jnp.sum(positions[:, None] * match, axis=0)
    gain_row = lax.dynamic_index_in_dim(hint_gain, layer_index[0], 0, keepdims=False)
    outgoing = jnp.take(control.reshape(owners, slab_rows, control.shape[1]), inverse, axis=0)
    arrived = lax.all_to_all(outgoing, "ulysses", split_axis=0, concat_axis=0, tiled=True).reshape(
        tok_rows, control.shape[1]
    )
    placed = make_hint(arrived, hint_weight)
    return (attended.astype(jnp.float32) + placed.astype(jnp.float32) * gain_row).astype(
        jnp.bfloat16
    )


def row_scale(values):
    return lax.rsqrt(jnp.mean(values * values, axis=-1, keepdims=True) + 1e-06)


def kernel(
    blks,
    owners,
    query_hbm,
    key_hbm,
    value_hbm,
    query_gain_hbm,
    key_gain_hbm,
    control_hbm,
    weight_hbm,
    gain_hbm,
    owner_smem,
    layer_smem,
    out_ref,
    query_in,
    key_in,
    value_in,
    query_gain,
    key_gain,
    control_in,
    weight,
    gains,
    stage,
    landed,
    passed,
    slabs_out,
    slabs_in,
    mixed_out,
    attended,
    hint,
    load_sem,
    send_sem,
    recv_sem,
    pass_send,
    pass_recv,
    slab_send,
    slab_recv,
    back_send,
    back_recv,
):
    rows = query_in.shape[0]
    cols = blks // CORES
    chips = cols * owners
    slab_rows = rows // owners
    b = lax.axis_index("blk")
    u = lax.axis_index("ulysses")
    parity = lax.rem(b, CORES)
    x = b // CORES
    me = x * owners + u
    partner = {"blk": x * CORES + (1 - parity)}

    loads = [
        pltpu.make_async_copy(source, target, load_sem.at[at])
        for at, (source, target) in enumerate(
            (
                (query_hbm, query_in),
                (query_gain_hbm, query_gain),
                (key_hbm, key_in),
                (key_gain_hbm, key_gain),
                (value_hbm, value_in),
                (control_hbm, control_in),
                (weight_hbm, weight),
                (gain_hbm, gains),
            )
        )
    ]
    for load in loads:
        load.start()

    others = []
    for dz in sorted(range(owners), key=lambda d: -min(d, owners - d)):
        for dx in reversed(range(cols)):
            if dx or dz:
                there_x = lax.rem(x + dx, cols)
                there_u = lax.rem(u + dz, owners)
                others.append(
                    (
                        there_x * owners + there_u,
                        {"blk": there_x * CORES + parity, "ulysses": there_u},
                    )
                )

    barrier = pltpu.get_barrier_semaphore()
    for _, device in others:
        pl.semaphore_signal(barrier, inc=1, device_id=device, device_id_type=MESH)
    pl.semaphore_signal(barrier, inc=1, device_id=partner, device_id_type=MESH)

    for first, gain, part in ((query_in, query_gain, 0), (key_in, key_gain, 1)):
        loads[2 * part].wait()
        loads[2 * part + 1].wait()
        values = first[...].astype(jnp.float32)
        normed = (values * row_scale(values) * gain[...]).astype(jnp.bfloat16)
        for h in range(chips):
            stage[h, part * rows : (part + 1) * rows] = normed[
                :, h * HEAD_DIM : (h + 1) * HEAD_DIM
            ]
    loads[4].wait()
    for h in range(chips):
        stage[h, 2 * rows :] = value_in[:, h * HEAD_DIM : (h + 1) * HEAD_DIM]

    loads[5].wait()
    values = control_in[...].astype(jnp.float32)
    normed = values * row_scale(values)
    pieces = [normed[j * slab_rows : (j + 1) * slab_rows] for j in range(owners)]
    for to in range(owners):
        picked = pieces[0]
        for j in range(1, owners):
            picked = jnp.where(owner_smem[0, j] == to, pieces[j], picked)
        slabs_out[to] = picked.astype(jnp.bfloat16)

    pl.semaphore_wait(barrier, len(others) + 1)

    started = []

    def send(source, target, sem_out, sem_in, device):
        copy = pltpu.make_async_remote_copy(
            src_ref=source,
            dst_ref=target,
            send_sem=sem_out,
            recv_sem=sem_in,
            device_id=device,
            device_id_type=MESH,
        )
        copy.start()
        started.append(copy)

    def arrive(target, sem_out, sem_in):
        pltpu.make_async_remote_copy(
            src_ref=target,
            dst_ref=target,
            send_sem=sem_out,
            recv_sem=sem_in,
            device_id=partner,
            device_id_type=MESH,
        ).wait_recv()

    for at, (there, device) in enumerate(others):
        send(stage.at[there], landed.at[me], send_sem.at[at], recv_sem.at[me], device)
    send(
        stage.at[me, pl.ds(rows, 2 * rows)],
        passed.at[me],
        pass_send.at[me],
        pass_recv.at[me],
        partner,
    )
    for d in range(1, owners):
        there = lax.rem(u + d, owners)
        send(
            slabs_out.at[there],
            slabs_in.at[u],
            slab_send.at[d],
            slab_recv.at[u],
            {"ulysses": there},
        )
    landed[me] = stage[me]
    slabs_in[u] = slabs_out[u]

    loads[6].wait()
    loads[7].wait()
    for d in range(1, owners):
        source = lax.rem(u + owners - d, owners)
        arrive(slabs_in.at[source], slab_send.at[0], slab_recv.at[source])
    arrived = slabs_in[...].astype(jnp.float32).reshape(rows, control_in.shape[1])
    placed = jnp.dot(
        arrived.astype(jnp.bfloat16), weight[...], preferred_element_type=jnp.float32
    ).astype(jnp.bfloat16)
    hint[...] = placed.astype(jnp.float32) * gains[pl.ds(layer_smem[0], 1), :]

    for there, _ in reversed(others):
        arrive(landed.at[there], pass_send.at[0], recv_sem.at[there])
        send(
            landed.at[there, pl.ds(rows, 2 * rows)],
            passed.at[there],
            pass_send.at[there],
            pass_recv.at[there],
            partner,
        )
    for there in [me] + [t for t, _ in reversed(others)]:
        arrive(passed.at[there], pass_send.at[0], pass_recv.at[there])

    count = chips * rows
    keys = jnp.concatenate(
        [
            landed[:, rows : 2 * rows].reshape(count, HEAD_DIM),
            passed[:, :rows].reshape(count, HEAD_DIM),
        ],
        axis=0,
    )
    mix = jnp.concatenate(
        [
            landed[:, 2 * rows :].reshape(count, HEAD_DIM),
            passed[:, rows:].reshape(count, HEAD_DIM),
        ],
        axis=0,
    )
    factor = HEAD_DIM ** (-0.5) * math.log2(math.e)
    targets = others + [(me, None)]
    group = max(1, chips // GROUPS)
    waiting = []

    def flush():
        for there, device, at in waiting:
            send(
                mixed_out.at[there],
                attended.at[me],
                back_send.at[at],
                back_recv.at[me],
                device,
            )
        waiting.clear()

    for base in range(0, chips, group):
        part = targets[base : base + group]
        queries = jnp.concatenate([landed[there, :rows] for there, _ in part], axis=0)
        scores = lax.dot_general(
            queries, keys, (((1,), (1,)), ((), ())), preferred_element_type=jnp.float32
        )
        peak = jnp.max(scores, axis=-1, keepdims=True)
        expo = jnp.exp2((scores - peak) * factor)
        totals = jnp.sum(expo, axis=-1, keepdims=True)
        output = jnp.dot(
            expo.astype(jnp.bfloat16), mix, preferred_element_type=jnp.float32
        )
        output = (output * (1.0 / totals)).astype(jnp.bfloat16)
        flush()
        for at, (there, device) in enumerate(part):
            piece = output[at * rows : (at + 1) * rows]
            if device is None:
                attended[there] = piece
            else:
                mixed_out[there] = piece
                waiting.append((there, device, base + at))
    flush()

    for there, _ in reversed(others):
        arrive(attended.at[there], back_send.at[0], back_recv.at[there])
    for h in range(chips):
        columns = slice(h * HEAD_DIM, (h + 1) * HEAD_DIM)
        out_ref[:, columns] = (attended[h].astype(jnp.float32) + hint[:, columns]).astype(
            jnp.bfloat16
        )
    for copy in started:
        copy.wait_send()


GROUPS = 2


def run(blks, owners, *arrays):
    query_proj, control, hint_weight, hint_gain = arrays[0], arrays[5], arrays[6], arrays[7]
    rows, feats = query_proj.shape
    chips = blks // CORES * owners
    fits = (
        blks % CORES == 0
        and chips * HEAD_DIM == feats
        and rows % 16 == 0
        and rows % owners == 0
        and (rows // owners) % 8 == 0
        and rows * chips <= 1024
    )
    if not fits:
        return shards(*arrays)
    inner = control.shape[1]
    dma = pltpu.SemaphoreType.DMA
    half = jnp.bfloat16
    wide = jnp.float32
    operands = list(arrays)
    operands[3] = arrays[3].reshape(1, feats)
    operands[4] = arrays[4].reshape(1, feats)
    return pl.pallas_call(
        functools.partial(kernel, blks, owners),
        out_shape=jax.ShapeDtypeStruct((rows, feats), half),
        in_specs=[pl.BlockSpec(memory_space=pl.ANY)] * 8
        + [pl.BlockSpec(memory_space=pltpu.SMEM)] * 2,
        out_specs=pl.BlockSpec(memory_space=pltpu.VMEM),
        scratch_shapes=[
            pltpu.VMEM((rows, feats), half),
            pltpu.VMEM((rows, feats), half),
            pltpu.VMEM((rows, feats), half),
            pltpu.VMEM((1, feats), wide),
            pltpu.VMEM((1, feats), wide),
            pltpu.VMEM((rows, inner), half),
            pltpu.VMEM(hint_weight.shape, half),
            pltpu.VMEM(hint_gain.shape, wide),
            pltpu.VMEM((chips, 3 * rows, HEAD_DIM), half),
            pltpu.VMEM((chips, 3 * rows, HEAD_DIM), half),
            pltpu.VMEM((chips, 2 * rows, HEAD_DIM), half),
            pltpu.VMEM((owners, rows // owners, inner), half),
            pltpu.VMEM((owners, rows // owners, inner), half),
            pltpu.VMEM((chips, rows, HEAD_DIM), half),
            pltpu.VMEM((chips, rows, HEAD_DIM), half),
            pltpu.VMEM((rows, feats), wide),
            dma((8,)),
            dma((chips,)),
            dma((chips,)),
            dma((chips,)),
            dma((chips,)),
            dma((owners,)),
            dma((owners,)),
            dma((chips,)),
            dma((chips,)),
        ],
        compiler_params=pltpu.CompilerParams(collective_id=0, has_side_effects=True),
    )(*operands)


def solution(mesh):
    return jax.shard_map(
        functools.partial(run, mesh.shape["blk"], mesh.shape["ulysses"]),
        mesh=mesh,
        in_specs=(
            P(("groups", "blk", "ulysses"), None),
            P(("groups", "blk", "ulysses"), None),
            P(("groups", "blk", "ulysses"), None),
            P(),
            P(),
            P(("groups", "blk", "ulysses"), None),
            P(),
            P(),
            P(("groups", "blk", "ulysses"), None),
            P(("groups", "blk", "ulysses")),
        ),
        out_specs=P(("groups", "blk", "ulysses"), None),
        check_vma=False,
    )
```

```python
import functools
import math

import jax
import jax.numpy as jnp
from jax import lax
from jax.experimental import pallas as pl
from jax.experimental.pallas import tpu as pltpu
from jax.sharding import PartitionSpec as P

HEAD_DIM = 128
CORES = 2
MESH = pl.DeviceIdType.MESH


def normalize_rows(rows, gain):
    values = rows.astype(jnp.float32)
    scale = lax.rsqrt(jnp.mean(values * values, axis=-1, keepdims=True) + 1e-06)
    return (values * scale * gain).astype(jnp.bfloat16)


def block_size(count):
    block = min(count, 1024)
    while count % block:
        block = block - 1
    return block


def make_fold(queries):
    rows = queries.shape[0]
    heads = queries.shape[1] // HEAD_DIM
    shaped = queries.reshape(rows, heads, HEAD_DIM)
    factor = HEAD_DIM ** (-0.5)

    def update(state, pair):
        peak, totals, accum = state
        key_block, value_block = pair
        scores = (
            jnp.einsum("qhd,khd->hqk", shaped, key_block, preferred_element_type=jnp.float32)
            * factor
        )
        new_peak = jnp.maximum(peak, jnp.max(scores, axis=-1))
        correction = jnp.exp(peak - new_peak)
        expo = jnp.exp(scores - new_peak[:, :, None])
        totals = totals * correction + jnp.sum(expo, axis=-1)
        mixed = jnp.einsum(
            "hqk,khd->hqd",
            expo.astype(jnp.bfloat16),
            value_block,
            preferred_element_type=jnp.float32,
        )
        accum = accum * correction[:, :, None] + mixed
        return ((new_peak, totals, accum), None)

    def fold(carry, piece, start):
        keys, values = piece
        count = keys.shape[0]
        block = block_size(count)
        key_blocks = keys.reshape(count // block, block, heads, HEAD_DIM)
        value_blocks = values.reshape(count // block, block, heads, HEAD_DIM)
        result, unused = lax.scan(update, carry, (key_blocks, value_blocks))
        return result

    start_state = (
        jnp.full((heads, rows), -1e30, jnp.float32),
        jnp.zeros((heads, rows), jnp.float32),
        jnp.zeros((heads, rows, HEAD_DIM), jnp.float32),
    )
    return (fold, start_state)


def finish(state):
    peak, totals, accum = state
    heads, rows = totals.shape
    output = (accum / totals[:, :, None]).astype(jnp.bfloat16)
    return output.transpose(1, 0, 2).reshape(rows, heads * HEAD_DIM)


def make_hint(patches, hint_weight):
    normed = normalize_rows(patches, jnp.float32(1.0))
    return jnp.dot(normed, hint_weight, preferred_element_type=jnp.float32).astype(jnp.bfloat16)


def shards(
    query_proj,
    key_proj,
    value_proj,
    query_gain,
    key_gain,
    control,
    hint_weight,
    hint_gain,
    owner_map,
    layer_index,
):
    query_normed = normalize_rows(query_proj, query_gain)
    key_normed = normalize_rows(key_proj, key_gain)
    query_heads, key_heads, value_heads = (
        lax.all_to_all(query_normed, "ulysses", split_axis=1, concat_axis=0, tiled=True),
        lax.all_to_all(key_normed, "ulysses", split_axis=1, concat_axis=0, tiled=True),
        lax.all_to_all(value_proj, "ulysses", split_axis=1, concat_axis=0, tiled=True),
    )
    fold, start_state = make_fold(query_heads)
    state = fold(
        start_state,
        (
            lax.all_gather(key_heads, "blk", axis=0, tiled=True),
            lax.all_gather(value_heads, "blk", axis=0, tiled=True),
        ),
        jnp.int32(0),
    )
    attended = lax.all_to_all(finish(state), "ulysses", split_axis=0, concat_axis=1, tiled=True)
    owners = lax.axis_size("ulysses")
    tok_rows = control.shape[0]
    slab_rows = tok_rows // owners
    positions = jnp.arange(owners, dtype=jnp.int32)
    match = (owner_map[0][:, None] == positions[None, :]).astype(jnp.int32)
    inverse = jnp.sum(positions[:, None] * match, axis=0)
    gain_row = lax.dynamic_index_in_dim(hint_gain, layer_index[0], 0, keepdims=False)
    outgoing = jnp.take(control.reshape(owners, slab_rows, control.shape[1]), inverse, axis=0)
    arrived = lax.all_to_all(outgoing, "ulysses", split_axis=0, concat_axis=0, tiled=True).reshape(
        tok_rows, control.shape[1]
    )
    placed = make_hint(arrived, hint_weight)
    return (attended.astype(jnp.float32) + placed.astype(jnp.float32) * gain_row).astype(
        jnp.bfloat16
    )


def row_scale(values):
    return lax.rsqrt(jnp.mean(values * values, axis=-1, keepdims=True) + 1e-06)


def kernel(
    blks,
    owners,
    query_hbm,
    key_hbm,
    value_hbm,
    query_gain_hbm,
    key_gain_hbm,
    control_hbm,
    weight_hbm,
    gain_hbm,
    owner_hbm,
    layer_smem,
    out_ref,
    query_in,
    key_in,
    value_in,
    query_gain,
    key_gain,
    control_in,
    weight,
    gains,
    owner_smem,
    stage,
    landed,
    passed,
    slabs_out,
    slabs_in,
    mixed_out,
    attended,
    hint,
    load_sem,
    send_sem,
    recv_sem,
    pass_send,
    pass_recv,
    slab_send,
    slab_recv,
    back_send,
    back_recv,
):
    rows = query_in.shape[0]
    cols = blks // CORES
    chips = cols * owners
    slab_rows = rows // owners
    b = lax.axis_index("blk")
    u = lax.axis_index("ulysses")
    parity = lax.rem(b, CORES)
    x = b // CORES
    me = x * owners + u
    partner = {"blk": x * CORES + (1 - parity)}

    loads = [
        pltpu.make_async_copy(source, target, load_sem.at[at])
        for at, (source, target) in enumerate(
            (
                (query_hbm, query_in),
                (query_gain_hbm, query_gain),
                (key_hbm, key_in),
                (key_gain_hbm, key_gain),
                (value_hbm, value_in),
                (control_hbm, control_in),
                (weight_hbm, weight),
                (gain_hbm, gains),
                (owner_hbm, owner_smem),
            )
        )
    ]
    for load in loads:
        load.start()

    others = []
    for dz in sorted(range(owners), key=lambda d: -min(d, owners - d)):
        for dx in reversed(range(cols)):
            if dx or dz:
                there_x = lax.rem(x + dx, cols)
                there_u = lax.rem(u + dz, owners)
                others.append(
                    (
                        there_x * owners + there_u,
                        {"blk": there_x * CORES + parity, "ulysses": there_u},
                    )
                )

    barrier = pltpu.get_barrier_semaphore()
    for _, device in others:
        pl.semaphore_signal(barrier, inc=1, device_id=device, device_id_type=MESH)
    pl.semaphore_signal(barrier, inc=1, device_id=partner, device_id_type=MESH)

    for first, gain, part in ((query_in, query_gain, 0), (key_in, key_gain, 1)):
        loads[2 * part].wait()
        loads[2 * part + 1].wait()
        values = first[...].astype(jnp.float32)
        normed = (values * row_scale(values) * gain[...]).astype(jnp.bfloat16)
        for h in range(chips):
            stage[h, part * rows : (part + 1) * rows] = normed[
                :, h * HEAD_DIM : (h + 1) * HEAD_DIM
            ]
    loads[4].wait()
    for h in range(chips):
        stage[h, 2 * rows :] = value_in[:, h * HEAD_DIM : (h + 1) * HEAD_DIM]

    loads[5].wait()
    loads[8].wait()
    values = control_in[...].astype(jnp.float32)
    normed = values * row_scale(values)
    pieces = [normed[j * slab_rows : (j + 1) * slab_rows] for j in range(owners)]
    for to in range(owners):
        picked = pieces[0]
        for j in range(1, owners):
            picked = jnp.where(owner_smem[0, j] == to, pieces[j], picked)
        slabs_out[to] = picked.astype(jnp.bfloat16)

    pl.semaphore_wait(barrier, len(others) + 1)

    started = []

    def send(source, target, sem_out, sem_in, device):
        copy = pltpu.make_async_remote_copy(
            src_ref=source,
            dst_ref=target,
            send_sem=sem_out,
            recv_sem=sem_in,
            device_id=device,
            device_id_type=MESH,
        )
        copy.start()
        started.append(copy)

    def arrive(target, sem_out, sem_in):
        pltpu.make_async_remote_copy(
            src_ref=target,
            dst_ref=target,
            send_sem=sem_out,
            recv_sem=sem_in,
            device_id=partner,
            device_id_type=MESH,
        ).wait_recv()

    for at, (there, device) in enumerate(others):
        send(stage.at[there], landed.at[me], send_sem.at[at], recv_sem.at[me], device)
    send(
        stage.at[me, pl.ds(rows, 2 * rows)],
        passed.at[me],
        pass_send.at[me],
        pass_recv.at[me],
        partner,
    )
    for d in range(1, owners):
        there = lax.rem(u + d, owners)
        send(
            slabs_out.at[there],
            slabs_in.at[u],
            slab_send.at[d],
            slab_recv.at[u],
            {"ulysses": there},
        )
    landed[me] = stage[me]
    slabs_in[u] = slabs_out[u]

    loads[6].wait()
    loads[7].wait()
    for d in range(1, owners):
        source = lax.rem(u + owners - d, owners)
        arrive(slabs_in.at[source], slab_send.at[0], slab_recv.at[source])
    arrived = slabs_in[...].astype(jnp.float32).reshape(rows, control_in.shape[1])
    placed = jnp.dot(
        arrived.astype(jnp.bfloat16), weight[...], preferred_element_type=jnp.float32
    ).astype(jnp.bfloat16)
    hint[...] = placed.astype(jnp.float32) * gains[pl.ds(layer_smem[0], 1), :]

    for there, _ in reversed(others):
        arrive(landed.at[there], pass_send.at[0], recv_sem.at[there])
        send(
            landed.at[there, pl.ds(rows, 2 * rows)],
            passed.at[there],
            pass_send.at[there],
            pass_recv.at[there],
            partner,
        )
    for there in [me] + [t for t, _ in reversed(others)]:
        arrive(passed.at[there], pass_send.at[0], pass_recv.at[there])

    count = chips * rows
    keys = jnp.concatenate(
        [
            landed[:, rows : 2 * rows].reshape(count, HEAD_DIM),
            passed[:, :rows].reshape(count, HEAD_DIM),
        ],
        axis=0,
    )
    mix = jnp.concatenate(
        [
            landed[:, 2 * rows :].reshape(count, HEAD_DIM),
            passed[:, rows:].reshape(count, HEAD_DIM),
        ],
        axis=0,
    )
    factor = HEAD_DIM ** (-0.5) * math.log2(math.e)
    targets = others + [(me, None)]
    group = max(1, chips // GROUPS)
    waiting = []

    def flush():
        for there, device, at in waiting:
            send(
                mixed_out.at[there],
                attended.at[me],
                back_send.at[at],
                back_recv.at[me],
                device,
            )
        waiting.clear()

    for base in range(0, chips, group):
        part = targets[base : base + group]
        queries = jnp.concatenate([landed[there, :rows] for there, _ in part], axis=0)
        scores = lax.dot_general(
            queries, keys, (((1,), (1,)), ((), ())), preferred_element_type=jnp.float32
        )
        peak = jnp.max(scores, axis=-1, keepdims=True)
        expo = jnp.exp2((scores - peak) * factor)
        totals = jnp.sum(expo, axis=-1, keepdims=True)
        output = jnp.dot(
            expo.astype(jnp.bfloat16), mix, preferred_element_type=jnp.float32
        )
        output = (output * (1.0 / totals)).astype(jnp.bfloat16)
        flush()
        for at, (there, device) in enumerate(part):
            piece = output[at * rows : (at + 1) * rows]
            if device is None:
                attended[there] = piece
            else:
                mixed_out[there] = piece
                waiting.append((there, device, base + at))
    flush()

    for there, _ in reversed(others):
        arrive(attended.at[there], back_send.at[0], back_recv.at[there])
    for h in range(chips):
        columns = slice(h * HEAD_DIM, (h + 1) * HEAD_DIM)
        out_ref[:, columns] = (attended[h].astype(jnp.float32) + hint[:, columns]).astype(
            jnp.bfloat16
        )
    for copy in started:
        copy.wait_send()


GROUPS = 2


def run(blks, owners, *arrays):
    query_proj, control, hint_weight, hint_gain = arrays[0], arrays[5], arrays[6], arrays[7]
    rows, feats = query_proj.shape
    chips = blks // CORES * owners
    fits = (
        blks % CORES == 0
        and chips * HEAD_DIM == feats
        and rows % 16 == 0
        and rows % owners == 0
        and (rows // owners) % 8 == 0
        and rows * chips <= 1024
    )
    if not fits:
        return shards(*arrays)
    inner = control.shape[1]
    dma = pltpu.SemaphoreType.DMA
    half = jnp.bfloat16
    wide = jnp.float32
    operands = list(arrays)
    operands[3] = arrays[3].reshape(1, feats)
    operands[4] = arrays[4].reshape(1, feats)
    layer = operands.pop()
    operands = [pltpu.with_memory_space_constraint(array, pltpu.HBM) for array in operands]
    return pl.pallas_call(
        functools.partial(kernel, blks, owners),
        out_shape=jax.ShapeDtypeStruct((rows, feats), half),
        in_specs=[pl.BlockSpec(memory_space=pltpu.HBM)] * len(operands)
        + [pl.BlockSpec(memory_space=pltpu.SMEM)],
        out_specs=pl.BlockSpec(memory_space=pltpu.VMEM),
        scratch_shapes=[
            pltpu.VMEM((rows, feats), half),
            pltpu.VMEM((rows, feats), half),
            pltpu.VMEM((rows, feats), half),
            pltpu.VMEM((1, feats), wide),
            pltpu.VMEM((1, feats), wide),
            pltpu.VMEM((rows, inner), half),
            pltpu.VMEM(hint_weight.shape, half),
            pltpu.VMEM(hint_gain.shape, wide),
            pltpu.SMEM((1, owners), jnp.int32),
            pltpu.VMEM((chips, 3 * rows, HEAD_DIM), half),
            pltpu.VMEM((chips, 3 * rows, HEAD_DIM), half),
            pltpu.VMEM((chips, 2 * rows, HEAD_DIM), half),
            pltpu.VMEM((owners, rows // owners, inner), half),
            pltpu.VMEM((owners, rows // owners, inner), half),
            pltpu.VMEM((chips, rows, HEAD_DIM), half),
            pltpu.VMEM((chips, rows, HEAD_DIM), half),
            pltpu.VMEM((rows, feats), wide),
            dma((len(operands),)),
            dma((chips,)),
            dma((chips,)),
            dma((chips,)),
            dma((chips,)),
            dma((owners,)),
            dma((owners,)),
            dma((chips,)),
            dma((chips,)),
        ],
        compiler_params=pltpu.CompilerParams(
            collective_id=0, has_side_effects=True, vmem_limit_bytes=16 << 20
        ),
    )(*operands, layer)


def solution(mesh):
    return jax.shard_map(
        functools.partial(run, mesh.shape["blk"], mesh.shape["ulysses"]),
        mesh=mesh,
        in_specs=(
            P(("groups", "blk", "ulysses"), None),
            P(("groups", "blk", "ulysses"), None),
            P(("groups", "blk", "ulysses"), None),
            P(),
            P(),
            P(("groups", "blk", "ulysses"), None),
            P(),
            P(),
            P(("groups", "blk", "ulysses"), None),
            P(("groups", "blk", "ulysses")),
        ),
        out_specs=P(("groups", "blk", "ulysses"), None),
        check_vma=False,
    )
```

```python
import functools
import math

import jax
import jax.numpy as jnp
from jax import lax
from jax.experimental import pallas as pl
from jax.experimental.pallas import tpu as pltpu
from jax.sharding import PartitionSpec as P

HEAD_DIM = 128
CORES = 2
MESH = pl.DeviceIdType.MESH


def normalize_rows(rows, gain):
    values = rows.astype(jnp.float32)
    scale = lax.rsqrt(jnp.mean(values * values, axis=-1, keepdims=True) + 1e-06)
    return (values * scale * gain).astype(jnp.bfloat16)


def block_size(count):
    block = min(count, 1024)
    while count % block:
        block = block - 1
    return block


def make_fold(queries):
    rows = queries.shape[0]
    heads = queries.shape[1] // HEAD_DIM
    shaped = queries.reshape(rows, heads, HEAD_DIM)
    factor = HEAD_DIM ** (-0.5)

    def update(state, pair):
        peak, totals, accum = state
        key_block, value_block = pair
        scores = (
            jnp.einsum("qhd,khd->hqk", shaped, key_block, preferred_element_type=jnp.float32)
            * factor
        )
        new_peak = jnp.maximum(peak, jnp.max(scores, axis=-1))
        correction = jnp.exp(peak - new_peak)
        expo = jnp.exp(scores - new_peak[:, :, None])
        totals = totals * correction + jnp.sum(expo, axis=-1)
        mixed = jnp.einsum(
            "hqk,khd->hqd",
            expo.astype(jnp.bfloat16),
            value_block,
            preferred_element_type=jnp.float32,
        )
        accum = accum * correction[:, :, None] + mixed
        return ((new_peak, totals, accum), None)

    def fold(carry, piece, start):
        keys, values = piece
        count = keys.shape[0]
        block = block_size(count)
        key_blocks = keys.reshape(count // block, block, heads, HEAD_DIM)
        value_blocks = values.reshape(count // block, block, heads, HEAD_DIM)
        result, unused = lax.scan(update, carry, (key_blocks, value_blocks))
        return result

    start_state = (
        jnp.full((heads, rows), -1e30, jnp.float32),
        jnp.zeros((heads, rows), jnp.float32),
        jnp.zeros((heads, rows, HEAD_DIM), jnp.float32),
    )
    return (fold, start_state)


def finish(state):
    peak, totals, accum = state
    heads, rows = totals.shape
    output = (accum / totals[:, :, None]).astype(jnp.bfloat16)
    return output.transpose(1, 0, 2).reshape(rows, heads * HEAD_DIM)


def make_hint(patches, hint_weight):
    normed = normalize_rows(patches, jnp.float32(1.0))
    return jnp.dot(normed, hint_weight, preferred_element_type=jnp.float32).astype(jnp.bfloat16)


def shards(
    query_proj,
    key_proj,
    value_proj,
    query_gain,
    key_gain,
    control,
    hint_weight,
    hint_gain,
    owner_map,
    layer_index,
):
    query_normed = normalize_rows(query_proj, query_gain)
    key_normed = normalize_rows(key_proj, key_gain)
    query_heads, key_heads, value_heads = (
        lax.all_to_all(query_normed, "ulysses", split_axis=1, concat_axis=0, tiled=True),
        lax.all_to_all(key_normed, "ulysses", split_axis=1, concat_axis=0, tiled=True),
        lax.all_to_all(value_proj, "ulysses", split_axis=1, concat_axis=0, tiled=True),
    )
    fold, start_state = make_fold(query_heads)
    state = fold(
        start_state,
        (
            lax.all_gather(key_heads, "blk", axis=0, tiled=True),
            lax.all_gather(value_heads, "blk", axis=0, tiled=True),
        ),
        jnp.int32(0),
    )
    attended = lax.all_to_all(finish(state), "ulysses", split_axis=0, concat_axis=1, tiled=True)
    owners = lax.axis_size("ulysses")
    tok_rows = control.shape[0]
    slab_rows = tok_rows // owners
    positions = jnp.arange(owners, dtype=jnp.int32)
    match = (owner_map[0][:, None] == positions[None, :]).astype(jnp.int32)
    inverse = jnp.sum(positions[:, None] * match, axis=0)
    gain_row = lax.dynamic_index_in_dim(hint_gain, layer_index[0], 0, keepdims=False)
    outgoing = jnp.take(control.reshape(owners, slab_rows, control.shape[1]), inverse, axis=0)
    arrived = lax.all_to_all(outgoing, "ulysses", split_axis=0, concat_axis=0, tiled=True).reshape(
        tok_rows, control.shape[1]
    )
    placed = make_hint(arrived, hint_weight)
    return (attended.astype(jnp.float32) + placed.astype(jnp.float32) * gain_row).astype(
        jnp.bfloat16
    )


def row_scale(values):
    return lax.rsqrt(jnp.mean(values * values, axis=-1, keepdims=True) + 1e-06)


def kernel(
    blks,
    owners,
    query_hbm,
    key_hbm,
    value_hbm,
    query_gain_hbm,
    key_gain_hbm,
    control_hbm,
    weight_hbm,
    gain_hbm,
    owner_hbm,
    layer_smem,
    out_ref,
    query_in,
    key_in,
    value_in,
    query_gain,
    key_gain,
    control_in,
    weight,
    gains,
    owner_smem,
    stage,
    landed,
    passed,
    slabs_out,
    slabs_in,
    mixed_out,
    attended,
    hint,
    load_sem,
    send_sem,
    recv_sem,
    pass_send,
    pass_recv,
    slab_send,
    slab_recv,
    back_send,
    back_recv,
    level_sem,
):
    rows = query_in.shape[0]
    cols = blks // CORES
    chips = cols * owners
    slab_rows = rows // owners
    b = lax.axis_index("blk")
    u = lax.axis_index("ulysses")
    parity = lax.rem(b, CORES)
    x = b // CORES
    me = x * owners + u
    partner = {"blk": x * CORES + (1 - parity)}

    loads = [
        pltpu.make_async_copy(source, target, load_sem.at[at])
        for at, (source, target) in enumerate(
            (
                (query_hbm, query_in),
                (query_gain_hbm, query_gain),
                (key_hbm, key_in),
                (key_gain_hbm, key_gain),
                (value_hbm, value_in),
                (control_hbm, control_in),
                (weight_hbm, weight),
                (gain_hbm, gains),
                (owner_hbm, owner_smem),
            )
        )
    ]
    for load in loads:
        load.start()

    others = []
    for dz in sorted(range(owners), key=lambda d: -min(d, owners - d)):
        for dx in reversed(range(cols)):
            if dx or dz:
                there_x = lax.rem(x + dx, cols)
                there_u = lax.rem(u + dz, owners)
                others.append(
                    (
                        there_x * owners + there_u,
                        {"blk": there_x * CORES + parity, "ulysses": there_u},
                    )
                )

    around = (
        (u > 0, {"ulysses": u - 1}),
        (u < owners - 1, {"ulysses": u + 1}),
        (x > 0, {"blk": b - CORES}),
        (x < cols - 1, {"blk": b + CORES}),
    )
    near = (
        (u + owners - 1) // owners
        + (2 * owners - 2 - u) // owners
        + (x + cols - 1) // cols
        + (2 * cols - 2 - x) // cols
    )

    def tell(semaphore):
        for inside, device in around:

            @pl.when(inside)
            def _():
                pl.semaphore_signal(
                    semaphore, inc=1, device_id=device, device_id_type=MESH
                )

    def ring(distance):
        for dz in range(-distance, distance + 1):
            for dx in sorted({abs(dz) - distance, distance - abs(dz)}):
                if abs(dx) < cols and abs(dz) < owners:
                    there_x, there_u = x + dx, u + dz
                    inside = (
                        (there_x >= 0)
                        & (there_x < cols)
                        & (there_u >= 0)
                        & (there_u < owners)
                    )
                    yield inside, there_x * owners + there_u, {
                        "blk": there_x * CORES + parity,
                        "ulysses": there_u,
                    }

    farthest = cols + owners - 2
    barrier = pltpu.get_barrier_semaphore()
    tell(barrier)
    pl.semaphore_signal(barrier, inc=1, device_id=partner, device_id_type=MESH)
    pl.semaphore_wait(barrier, near + 1)
    if farthest > 1:
        tell(level_sem.at[2])

    for first, gain, part in ((query_in, query_gain, 0), (key_in, key_gain, 1)):
        loads[2 * part].wait()
        loads[2 * part + 1].wait()
        values = first[...].astype(jnp.float32)
        normed = (values * row_scale(values) * gain[...]).astype(jnp.bfloat16)
        for h in range(chips):
            stage[h, part * rows : (part + 1) * rows] = normed[
                :, h * HEAD_DIM : (h + 1) * HEAD_DIM
            ]
    loads[4].wait()
    for h in range(chips):
        stage[h, 2 * rows :] = value_in[:, h * HEAD_DIM : (h + 1) * HEAD_DIM]

    started = []

    def remote(source, target, sem_out, sem_in, device):
        return pltpu.make_async_remote_copy(
            src_ref=source,
            dst_ref=target,
            send_sem=sem_out,
            recv_sem=sem_in,
            device_id=device,
            device_id_type=MESH,
        )

    def send(*way):
        copy = remote(*way)
        copy.start()
        started.append(copy)

    def arrive(target, sem_out, sem_in):
        pltpu.make_async_remote_copy(
            src_ref=target,
            dst_ref=target,
            send_sem=sem_out,
            recv_sem=sem_in,
            device_id=partner,
            device_id_type=MESH,
        ).wait_recv()

    send(
        stage.at[me, pl.ds(rows, 2 * rows)],
        passed.at[me],
        pass_send.at[me],
        pass_recv.at[me],
        partner,
    )
    for distance in range(1, farthest + 1):
        if distance > 1:
            pl.semaphore_wait(level_sem.at[distance], near)
            if distance < farthest:
                tell(level_sem.at[distance + 1])
        for inside, there, device in ring(distance):

            @pl.when(inside)
            def _():
                remote(
                    stage.at[there], landed.at[me], send_sem.at[there], recv_sem.at[me], device
                ).start()

    loads[5].wait()
    loads[8].wait()
    values = control_in[...].astype(jnp.float32)
    normed = values * row_scale(values)
    pieces = [normed[j * slab_rows : (j + 1) * slab_rows] for j in range(owners)]
    for to in range(owners):
        picked = pieces[0]
        for j in range(1, owners):
            picked = jnp.where(owner_smem[0, j] == to, pieces[j], picked)
        slabs_out[to] = picked.astype(jnp.bfloat16)

    for d in range(1, owners):
        there = lax.rem(u + d, owners)
        send(
            slabs_out.at[there],
            slabs_in.at[u],
            slab_send.at[d],
            slab_recv.at[u],
            {"ulysses": there},
        )
    landed[me] = stage[me]
    slabs_in[u] = slabs_out[u]

    for distance in range(1, farthest + 1):
        for inside, there, _ in ring(distance):

            @pl.when(inside)
            def _():
                arrive(landed.at[there], pass_send.at[0], recv_sem.at[there])
                remote(
                    landed.at[there, pl.ds(rows, 2 * rows)],
                    passed.at[there],
                    pass_send.at[there],
                    pass_recv.at[there],
                    partner,
                ).start()

    for there in [me] + [t for t, _ in reversed(others)]:
        arrive(passed.at[there], pass_send.at[0], pass_recv.at[there])

    count = chips * rows
    keys = jnp.concatenate(
        [
            landed[:, rows : 2 * rows].reshape(count, HEAD_DIM),
            passed[:, :rows].reshape(count, HEAD_DIM),
        ],
        axis=0,
    )
    mix = jnp.concatenate(
        [
            landed[:, 2 * rows :].reshape(count, HEAD_DIM),
            passed[:, rows:].reshape(count, HEAD_DIM),
        ],
        axis=0,
    )
    factor = HEAD_DIM ** (-0.5) * math.log2(math.e)
    targets = others + [(me, None)]
    group = max(1, chips // GROUPS)
    waiting = []

    def flush():
        for there, device, at in waiting:
            send(
                mixed_out.at[there],
                attended.at[me],
                back_send.at[at],
                back_recv.at[me],
                device,
            )
        waiting.clear()

    for base in range(0, chips, group):
        part = targets[base : base + group]
        queries = jnp.concatenate([landed[there, :rows] for there, _ in part], axis=0)
        scores = lax.dot_general(
            queries, keys, (((1,), (1,)), ((), ())), preferred_element_type=jnp.float32
        )
        peak = jnp.max(scores, axis=-1, keepdims=True)
        expo = jnp.exp2((scores - peak) * factor)
        totals = jnp.sum(expo, axis=-1, keepdims=True)
        output = jnp.dot(
            expo.astype(jnp.bfloat16), mix, preferred_element_type=jnp.float32
        )
        output = (output * (1.0 / totals)).astype(jnp.bfloat16)
        flush()
        for at, (there, device) in enumerate(part):
            piece = output[at * rows : (at + 1) * rows]
            if device is None:
                attended[there] = piece
            else:
                mixed_out[there] = piece
                waiting.append((there, device, base + at))
    flush()

    loads[6].wait()
    loads[7].wait()
    for d in range(1, owners):
        source = lax.rem(u + owners - d, owners)
        arrive(slabs_in.at[source], slab_send.at[0], slab_recv.at[source])
    arrived = slabs_in[...].astype(jnp.float32).reshape(rows, control_in.shape[1])
    placed = jnp.dot(
        arrived.astype(jnp.bfloat16), weight[...], preferred_element_type=jnp.float32
    ).astype(jnp.bfloat16)
    hint[...] = placed.astype(jnp.float32) * gains[pl.ds(layer_smem[0], 1), :]

    for there, _ in reversed(others):
        arrive(attended.at[there], back_send.at[0], back_recv.at[there])
    for h in range(chips):
        columns = slice(h * HEAD_DIM, (h + 1) * HEAD_DIM)
        out_ref[:, columns] = (attended[h].astype(jnp.float32) + hint[:, columns]).astype(
            jnp.bfloat16
        )
    for there, device in others:
        started.append(
            remote(stage.at[there], landed.at[me], send_sem.at[there], recv_sem.at[me], device)
        )
        started.append(
            remote(
                landed.at[there, pl.ds(rows, 2 * rows)],
                passed.at[there],
                pass_send.at[there],
                pass_recv.at[there],
                partner,
            )
        )
    for copy in started:
        copy.wait_send()


GROUPS = 2


def run(blks, owners, *arrays):
    query_proj, control, hint_weight, hint_gain = arrays[0], arrays[5], arrays[6], arrays[7]
    rows, feats = query_proj.shape
    chips = blks // CORES * owners
    fits = (
        blks % CORES == 0
        and chips * HEAD_DIM == feats
        and rows % 16 == 0
        and rows % owners == 0
        and (rows // owners) % 8 == 0
        and rows * chips <= 1024
    )
    if not fits:
        return shards(*arrays)
    inner = control.shape[1]
    dma = pltpu.SemaphoreType.DMA
    half = jnp.bfloat16
    wide = jnp.float32
    operands = list(arrays)
    operands[3] = arrays[3].reshape(1, feats)
    operands[4] = arrays[4].reshape(1, feats)
    layer = operands.pop()
    operands = [pltpu.with_memory_space_constraint(array, pltpu.HBM) for array in operands]
    return pl.pallas_call(
        functools.partial(kernel, blks, owners),
        out_shape=jax.ShapeDtypeStruct((rows, feats), half),
        in_specs=[pl.BlockSpec(memory_space=pltpu.HBM)] * len(operands)
        + [pl.BlockSpec(memory_space=pltpu.SMEM)],
        out_specs=pl.BlockSpec(memory_space=pltpu.VMEM),
        scratch_shapes=[
            pltpu.VMEM((rows, feats), half),
            pltpu.VMEM((rows, feats), half),
            pltpu.VMEM((rows, feats), half),
            pltpu.VMEM((1, feats), wide),
            pltpu.VMEM((1, feats), wide),
            pltpu.VMEM((rows, inner), half),
            pltpu.VMEM(hint_weight.shape, half),
            pltpu.VMEM(hint_gain.shape, wide),
            pltpu.SMEM((1, owners), jnp.int32),
            pltpu.VMEM((chips, 3 * rows, HEAD_DIM), half),
            pltpu.VMEM((chips, 3 * rows, HEAD_DIM), half),
            pltpu.VMEM((chips, 2 * rows, HEAD_DIM), half),
            pltpu.VMEM((owners, rows // owners, inner), half),
            pltpu.VMEM((owners, rows // owners, inner), half),
            pltpu.VMEM((chips, rows, HEAD_DIM), half),
            pltpu.VMEM((chips, rows, HEAD_DIM), half),
            pltpu.VMEM((rows, feats), wide),
            dma((len(operands),)),
            dma((chips,)),
            dma((chips,)),
            dma((chips,)),
            dma((chips,)),
            dma((owners,)),
            dma((owners,)),
            dma((chips,)),
            dma((chips,)),
            pltpu.SemaphoreType.REGULAR((blks // CORES + owners,)),
        ],
        compiler_params=pltpu.CompilerParams(
            collective_id=0, has_side_effects=True, vmem_limit_bytes=16 << 20
        ),
    )(*operands, layer)


def solution(mesh):
    return jax.shard_map(
        functools.partial(run, mesh.shape["blk"], mesh.shape["ulysses"]),
        mesh=mesh,
        in_specs=(
            P(("groups", "blk", "ulysses"), None),
            P(("groups", "blk", "ulysses"), None),
            P(("groups", "blk", "ulysses"), None),
            P(),
            P(),
            P(("groups", "blk", "ulysses"), None),
            P(),
            P(),
            P(("groups", "blk", "ulysses"), None),
            P(("groups", "blk", "ulysses")),
        ),
        out_specs=P(("groups", "blk", "ulysses"), None),
        check_vma=False,
    )
```

```python
import functools
import math

import jax
import jax.numpy as jnp
from jax import lax
from jax.experimental import pallas as pl
from jax.experimental.pallas import tpu as pltpu
from jax.sharding import PartitionSpec as P

HEAD_DIM = 128
CORES = 2
MESH = pl.DeviceIdType.MESH


def normalize_rows(rows, gain):
    values = rows.astype(jnp.float32)
    scale = lax.rsqrt(jnp.mean(values * values, axis=-1, keepdims=True) + 1e-06)
    return (values * scale * gain).astype(jnp.bfloat16)


def block_size(count):
    block = min(count, 1024)
    while count % block:
        block = block - 1
    return block


def make_fold(queries):
    rows = queries.shape[0]
    heads = queries.shape[1] // HEAD_DIM
    shaped = queries.reshape(rows, heads, HEAD_DIM)
    factor = HEAD_DIM ** (-0.5)

    def update(state, pair):
        peak, totals, accum = state
        key_block, value_block = pair
        scores = (
            jnp.einsum("qhd,khd->hqk", shaped, key_block, preferred_element_type=jnp.float32)
            * factor
        )
        new_peak = jnp.maximum(peak, jnp.max(scores, axis=-1))
        correction = jnp.exp(peak - new_peak)
        expo = jnp.exp(scores - new_peak[:, :, None])
        totals = totals * correction + jnp.sum(expo, axis=-1)
        mixed = jnp.einsum(
            "hqk,khd->hqd",
            expo.astype(jnp.bfloat16),
            value_block,
            preferred_element_type=jnp.float32,
        )
        accum = accum * correction[:, :, None] + mixed
        return ((new_peak, totals, accum), None)

    def fold(carry, piece, start):
        keys, values = piece
        count = keys.shape[0]
        block = block_size(count)
        key_blocks = keys.reshape(count // block, block, heads, HEAD_DIM)
        value_blocks = values.reshape(count // block, block, heads, HEAD_DIM)
        result, unused = lax.scan(update, carry, (key_blocks, value_blocks))
        return result

    start_state = (
        jnp.full((heads, rows), -1e30, jnp.float32),
        jnp.zeros((heads, rows), jnp.float32),
        jnp.zeros((heads, rows, HEAD_DIM), jnp.float32),
    )
    return (fold, start_state)


def finish(state):
    peak, totals, accum = state
    heads, rows = totals.shape
    output = (accum / totals[:, :, None]).astype(jnp.bfloat16)
    return output.transpose(1, 0, 2).reshape(rows, heads * HEAD_DIM)


def make_hint(patches, hint_weight):
    normed = normalize_rows(patches, jnp.float32(1.0))
    return jnp.dot(normed, hint_weight, preferred_element_type=jnp.float32).astype(jnp.bfloat16)


def shards(
    query_proj,
    key_proj,
    value_proj,
    query_gain,
    key_gain,
    control,
    hint_weight,
    hint_gain,
    owner_map,
    layer_index,
):
    query_normed = normalize_rows(query_proj, query_gain)
    key_normed = normalize_rows(key_proj, key_gain)
    query_heads, key_heads, value_heads = (
        lax.all_to_all(query_normed, "ulysses", split_axis=1, concat_axis=0, tiled=True),
        lax.all_to_all(key_normed, "ulysses", split_axis=1, concat_axis=0, tiled=True),
        lax.all_to_all(value_proj, "ulysses", split_axis=1, concat_axis=0, tiled=True),
    )
    fold, start_state = make_fold(query_heads)
    state = fold(
        start_state,
        (
            lax.all_gather(key_heads, "blk", axis=0, tiled=True),
            lax.all_gather(value_heads, "blk", axis=0, tiled=True),
        ),
        jnp.int32(0),
    )
    attended = lax.all_to_all(finish(state), "ulysses", split_axis=0, concat_axis=1, tiled=True)
    owners = lax.axis_size("ulysses")
    tok_rows = control.shape[0]
    slab_rows = tok_rows // owners
    positions = jnp.arange(owners, dtype=jnp.int32)
    match = (owner_map[0][:, None] == positions[None, :]).astype(jnp.int32)
    inverse = jnp.sum(positions[:, None] * match, axis=0)
    gain_row = lax.dynamic_index_in_dim(hint_gain, layer_index[0], 0, keepdims=False)
    outgoing = jnp.take(control.reshape(owners, slab_rows, control.shape[1]), inverse, axis=0)
    arrived = lax.all_to_all(outgoing, "ulysses", split_axis=0, concat_axis=0, tiled=True).reshape(
        tok_rows, control.shape[1]
    )
    placed = make_hint(arrived, hint_weight)
    return (attended.astype(jnp.float32) + placed.astype(jnp.float32) * gain_row).astype(
        jnp.bfloat16
    )


def row_scale(values):
    return lax.rsqrt(jnp.mean(values * values, axis=-1, keepdims=True) + 1e-06)


def kernel(
    blks,
    owners,
    query_hbm,
    key_hbm,
    value_hbm,
    query_gain_hbm,
    key_gain_hbm,
    control_hbm,
    weight_hbm,
    gain_hbm,
    owner_hbm,
    layer_smem,
    out_ref,
    query_in,
    key_in,
    value_in,
    query_gain,
    key_gain,
    control_in,
    weight,
    gains,
    owner_smem,
    stage,
    landed,
    slabs_out,
    slabs_in,
    mixed_out,
    attended,
    hint,
    load_sem,
    send_sem,
    recv_sem,
    slab_send,
    slab_recv,
    back_send,
    back_recv,
    level_sem,
):
    rows = query_in.shape[0]
    low, high = host_range(owners)
    wide = high - low
    heads = blks * wide
    cols = blks // CORES
    devices = blks * owners
    slab_rows = rows // owners
    b = lax.axis_index("blk")
    u = lax.axis_index("ulysses")
    parity = lax.rem(b, CORES)
    x = b // CORES
    me = b * owners + u
    own = b * wide + u - low
    hosting = (u >= low) & (u < high)

    loads = [
        pltpu.make_async_copy(source, target, load_sem.at[at])
        for at, (source, target) in enumerate(
            (
                (query_hbm, query_in),
                (query_gain_hbm, query_gain),
                (key_hbm, key_in),
                (key_gain_hbm, key_gain),
                (value_hbm, value_in),
                (control_hbm, control_in),
                (weight_hbm, weight),
                (gain_hbm, gains),
                (owner_hbm, owner_smem),
            )
        )
    ]
    for load in loads:
        load.start()

    around = (
        (b >= 0, {"blk": x * CORES + (1 - parity)}),
        (u > 0, {"ulysses": u - 1}),
        (u < owners - 1, {"ulysses": u + 1}),
        (x > 0, {"blk": b - CORES}),
        (x < cols - 1, {"blk": b + CORES}),
    )
    near = (
        1
        + (u + owners - 1) // owners
        + (2 * owners - 2 - u) // owners
        + (x + cols - 1) // cols
        + (2 * cols - 2 - x) // cols
    )

    def tell(semaphore):
        for inside, device in around:

            @pl.when(inside)
            def _():
                pl.semaphore_signal(
                    semaphore, inc=1, device_id=device, device_id_type=MESH
                )

    def hops(to_b, to_u):
        return (
            jnp.abs(to_b // CORES - x) + jnp.abs(to_b % CORES - parity) + jnp.abs(to_u - u)
        )

    reach = max(max(high - 1, owners - 1 - low) + cols, owners - 1)
    barrier = pltpu.get_barrier_semaphore()
    tell(barrier)
    pl.semaphore_wait(barrier, near)
    tell(level_sem.at[2])

    for first, gain, part in ((query_in, query_gain, 0), (key_in, key_gain, 1)):
        loads[2 * part].wait()
        loads[2 * part + 1].wait()
        values = first[...].astype(jnp.float32)
        normed = (values * row_scale(values) * gain[...]).astype(jnp.bfloat16)
        for h in range(heads):
            stage[h, part * rows : (part + 1) * rows] = normed[
                :, h * HEAD_DIM : (h + 1) * HEAD_DIM
            ]
    loads[4].wait()
    for h in range(heads):
        stage[h, 2 * rows :] = value_in[:, h * HEAD_DIM : (h + 1) * HEAD_DIM]

    started = []

    def remote(source, target, sem_out, sem_in, device):
        return pltpu.make_async_remote_copy(
            src_ref=source,
            dst_ref=target,
            send_sem=sem_out,
            recv_sem=sem_in,
            device_id=device,
            device_id_type=MESH,
        )

    def send(*way):
        copy = remote(*way)
        copy.start()
        started.append(copy)

    def arrive(target, sem_out, sem_in):
        pltpu.make_async_remote_copy(
            src_ref=target,
            dst_ref=target,
            send_sem=sem_out,
            recv_sem=sem_in,
            device_id={"blk": x * CORES + (1 - parity)},
            device_id_type=MESH,
        ).wait_recv()

    hosts = [(h, h // wide, low + h % wide) for h in range(heads)]
    for distance in range(1, reach + 1):
        if distance > 1:
            pl.semaphore_wait(level_sem.at[distance], near)
            if distance < reach:
                tell(level_sem.at[distance + 1])
        for h, to_b, to_u in hosts:

            @pl.when(hops(to_b, to_u) == distance)
            def _():
                remote(
                    stage.at[h],
                    landed.at[me],
                    send_sem.at[h],
                    recv_sem.at[me],
                    {"blk": to_b, "ulysses": to_u},
                ).start()

    loads[5].wait()
    loads[8].wait()
    values = control_in[...].astype(jnp.float32)
    normed = values * row_scale(values)
    pieces = [normed[j * slab_rows : (j + 1) * slab_rows] for j in range(owners)]
    for to in range(owners):
        picked = pieces[0]
        for j in range(1, owners):
            picked = jnp.where(owner_smem[0, j] == to, pieces[j], picked)
        slabs_out[to] = picked.astype(jnp.bfloat16)

    for d in range(1, owners):
        there = lax.rem(u + d, owners)
        send(
            slabs_out.at[there],
            slabs_in.at[u],
            slab_send.at[d],
            slab_recv.at[u],
            {"ulysses": there},
        )
    slabs_in[u] = slabs_out[u]

    order = [
        (to_b, to_u)
        for to_u in sorted(range(owners), key=lambda at: (low <= at < high, at))
        for to_b in range(blks)
    ]
    factor = HEAD_DIM ** (-0.5) * math.log2(math.e)

    @pl.when(hosting)
    def _():
        landed[me] = stage[own]
        for to_b, to_u in order:
            there = to_b * owners + to_u

            @pl.when(there != me)
            def _():
                arrive(landed.at[there], back_send.at[0], recv_sem.at[there])

        count = devices * rows
        keys = landed[:, rows : 2 * rows].reshape(count, HEAD_DIM)
        mix = landed[:, 2 * rows :].reshape(count, HEAD_DIM)
        group = devices // GROUPS

        def flush(base):
            for to_b, to_u in order[base : base + group]:
                there = to_b * owners + to_u

                @pl.when(there != me)
                def _():
                    remote(
                        mixed_out.at[there],
                        attended.at[own],
                        back_send.at[there],
                        back_recv.at[own],
                        {"blk": to_b, "ulysses": to_u},
                    ).start()

        for base in range(0, devices, group):
            part = [to_b * owners + to_u for to_b, to_u in order[base : base + group]]
            queries = jnp.concatenate([landed[there, :rows] for there in part], axis=0)
            scores = lax.dot_general(
                queries, keys, (((1,), (1,)), ((), ())), preferred_element_type=jnp.float32
            )
            peak = jnp.max(scores, axis=-1, keepdims=True)
            expo = jnp.exp2((scores - peak) * factor)
            totals = jnp.sum(expo, axis=-1, keepdims=True)
            output = jnp.dot(
                expo.astype(jnp.bfloat16), mix, preferred_element_type=jnp.float32
            )
            output = (output * (1.0 / totals)).astype(jnp.bfloat16)
            if base:
                flush(base - group)
            for at, there in enumerate(part):
                mixed_out[there] = output[at * rows : (at + 1) * rows]
        flush(devices - group)
        attended[own] = mixed_out[me]

    loads[6].wait()
    loads[7].wait()
    for d in range(1, owners):
        source = lax.rem(u + owners - d, owners)
        arrive(slabs_in.at[source], slab_send.at[0], slab_recv.at[source])
    arrived = slabs_in[...].astype(jnp.float32).reshape(rows, control_in.shape[1])
    placed = jnp.dot(
        arrived.astype(jnp.bfloat16), weight[...], preferred_element_type=jnp.float32
    ).astype(jnp.bfloat16)
    hint[...] = placed.astype(jnp.float32) * gains[pl.ds(layer_smem[0], 1), :]

    for h, to_b, to_u in hosts:

        @pl.when(hops(to_b, to_u) > 0)
        def _():
            arrive(attended.at[h], back_send.at[0], back_recv.at[h])
            remote(
                stage.at[h], landed.at[me], send_sem.at[h], recv_sem.at[me], around[0][1]
            ).wait_send()

    for h in range(heads):
        columns = slice(h * HEAD_DIM, (h + 1) * HEAD_DIM)
        out_ref[:, columns] = (attended[h].astype(jnp.float32) + hint[:, columns]).astype(
            jnp.bfloat16
        )
    for copy in started:
        copy.wait_send()

    @pl.when(hosting)
    def _():
        for there in range(devices):

            @pl.when(there != me)
            def _():
                remote(
                    mixed_out.at[there],
                    attended.at[own],
                    back_send.at[there],
                    back_recv.at[own],
                    around[0][1],
                ).wait_send()


GROUPS = 4


def host_range(owners):
    low = owners // 4
    return (low, owners - low)


def run(blks, owners, *arrays):
    query_proj, control, hint_weight, hint_gain = arrays[0], arrays[5], arrays[6], arrays[7]
    rows, feats = query_proj.shape
    low, high = host_range(owners)
    heads = blks * (high - low)
    devices = blks * owners
    fits = (
        blks % CORES == 0
        and owners > 1
        and heads * HEAD_DIM == feats
        and devices % GROUPS == 0
        and rows % 16 == 0
        and rows % owners == 0
        and (rows // owners) % 8 == 0
        and rows * devices <= 1024
    )
    if not fits:
        return shards(*arrays)
    inner = control.shape[1]
    dma = pltpu.SemaphoreType.DMA
    half = jnp.bfloat16
    wide = jnp.float32
    operands = list(arrays)
    operands[3] = arrays[3].reshape(1, feats)
    operands[4] = arrays[4].reshape(1, feats)
    layer = operands.pop()
    operands = [pltpu.with_memory_space_constraint(array, pltpu.HBM) for array in operands]
    return pl.pallas_call(
        functools.partial(kernel, blks, owners),
        out_shape=jax.ShapeDtypeStruct((rows, feats), half),
        in_specs=[pl.BlockSpec(memory_space=pltpu.HBM)] * len(operands)
        + [pl.BlockSpec(memory_space=pltpu.SMEM)],
        out_specs=pl.BlockSpec(memory_space=pltpu.VMEM),
        scratch_shapes=[
            pltpu.VMEM((rows, feats), half),
            pltpu.VMEM((rows, feats), half),
            pltpu.VMEM((rows, feats), half),
            pltpu.VMEM((1, feats), wide),
            pltpu.VMEM((1, feats), wide),
            pltpu.VMEM((rows, inner), half),
            pltpu.VMEM(hint_weight.shape, half),
            pltpu.VMEM(hint_gain.shape, wide),
            pltpu.SMEM((1, owners), jnp.int32),
            pltpu.VMEM((heads, 3 * rows, HEAD_DIM), half),
            pltpu.VMEM((devices, 3 * rows, HEAD_DIM), half),
            pltpu.VMEM((owners, rows // owners, inner), half),
            pltpu.VMEM((owners, rows // owners, inner), half),
            pltpu.VMEM((devices, rows, HEAD_DIM), half),
            pltpu.VMEM((heads, rows, HEAD_DIM), half),
            pltpu.VMEM((rows, feats), wide),
            dma((len(operands),)),
            dma((heads,)),
            dma((devices,)),
            dma((owners,)),
            dma((owners,)),
            dma((devices,)),
            dma((heads,)),
            pltpu.SemaphoreType.REGULAR((blks // CORES + owners + 1,)),
        ],
        compiler_params=pltpu.CompilerParams(
            collective_id=0, has_side_effects=True, vmem_limit_bytes=16 << 20
        ),
    )(*operands, layer)


def solution(mesh):
    return jax.shard_map(
        functools.partial(run, mesh.shape["blk"], mesh.shape["ulysses"]),
        mesh=mesh,
        in_specs=(
            P(("groups", "blk", "ulysses"), None),
            P(("groups", "blk", "ulysses"), None),
            P(("groups", "blk", "ulysses"), None),
            P(),
            P(),
            P(("groups", "blk", "ulysses"), None),
            P(),
            P(),
            P(("groups", "blk", "ulysses"), None),
            P(("groups", "blk", "ulysses")),
        ),
        out_specs=P(("groups", "blk", "ulysses"), None),
        check_vma=False,
    )
```

```python
import functools
import math

import jax
import jax.numpy as jnp
from jax import lax
from jax.experimental import pallas as pl
from jax.experimental.pallas import tpu as pltpu
from jax.sharding import PartitionSpec as P

HEAD_DIM = 128
CORES = 2
MESH = pl.DeviceIdType.MESH


def normalize_rows(rows, gain):
    values = rows.astype(jnp.float32)
    scale = lax.rsqrt(jnp.mean(values * values, axis=-1, keepdims=True) + 1e-06)
    return (values * scale * gain).astype(jnp.bfloat16)


def block_size(count):
    block = min(count, 1024)
    while count % block:
        block = block - 1
    return block


def make_fold(queries):
    rows = queries.shape[0]
    heads = queries.shape[1] // HEAD_DIM
    shaped = queries.reshape(rows, heads, HEAD_DIM)
    factor = HEAD_DIM ** (-0.5)

    def update(state, pair):
        peak, totals, accum = state
        key_block, value_block = pair
        scores = (
            jnp.einsum("qhd,khd->hqk", shaped, key_block, preferred_element_type=jnp.float32)
            * factor
        )
        new_peak = jnp.maximum(peak, jnp.max(scores, axis=-1))
        correction = jnp.exp(peak - new_peak)
        expo = jnp.exp(scores - new_peak[:, :, None])
        totals = totals * correction + jnp.sum(expo, axis=-1)
        mixed = jnp.einsum(
            "hqk,khd->hqd",
            expo.astype(jnp.bfloat16),
            value_block,
            preferred_element_type=jnp.float32,
        )
        accum = accum * correction[:, :, None] + mixed
        return ((new_peak, totals, accum), None)

    def fold(carry, piece, start):
        keys, values = piece
        count = keys.shape[0]
        block = block_size(count)
        key_blocks = keys.reshape(count // block, block, heads, HEAD_DIM)
        value_blocks = values.reshape(count // block, block, heads, HEAD_DIM)
        result, unused = lax.scan(update, carry, (key_blocks, value_blocks))
        return result

    start_state = (
        jnp.full((heads, rows), -1e30, jnp.float32),
        jnp.zeros((heads, rows), jnp.float32),
        jnp.zeros((heads, rows, HEAD_DIM), jnp.float32),
    )
    return (fold, start_state)


def finish(state):
    peak, totals, accum = state
    heads, rows = totals.shape
    output = (accum / totals[:, :, None]).astype(jnp.bfloat16)
    return output.transpose(1, 0, 2).reshape(rows, heads * HEAD_DIM)


def make_hint(patches, hint_weight):
    normed = normalize_rows(patches, jnp.float32(1.0))
    return jnp.dot(normed, hint_weight, preferred_element_type=jnp.float32).astype(jnp.bfloat16)


def shards(
    query_proj,
    key_proj,
    value_proj,
    query_gain,
    key_gain,
    control,
    hint_weight,
    hint_gain,
    owner_map,
    layer_index,
):
    query_normed = normalize_rows(query_proj, query_gain)
    key_normed = normalize_rows(key_proj, key_gain)
    query_heads, key_heads, value_heads = (
        lax.all_to_all(query_normed, "ulysses", split_axis=1, concat_axis=0, tiled=True),
        lax.all_to_all(key_normed, "ulysses", split_axis=1, concat_axis=0, tiled=True),
        lax.all_to_all(value_proj, "ulysses", split_axis=1, concat_axis=0, tiled=True),
    )
    fold, start_state = make_fold(query_heads)
    state = fold(
        start_state,
        (
            lax.all_gather(key_heads, "blk", axis=0, tiled=True),
            lax.all_gather(value_heads, "blk", axis=0, tiled=True),
        ),
        jnp.int32(0),
    )
    attended = lax.all_to_all(finish(state), "ulysses", split_axis=0, concat_axis=1, tiled=True)
    owners = lax.axis_size("ulysses")
    tok_rows = control.shape[0]
    slab_rows = tok_rows // owners
    positions = jnp.arange(owners, dtype=jnp.int32)
    match = (owner_map[0][:, None] == positions[None, :]).astype(jnp.int32)
    inverse = jnp.sum(positions[:, None] * match, axis=0)
    gain_row = lax.dynamic_index_in_dim(hint_gain, layer_index[0], 0, keepdims=False)
    outgoing = jnp.take(control.reshape(owners, slab_rows, control.shape[1]), inverse, axis=0)
    arrived = lax.all_to_all(outgoing, "ulysses", split_axis=0, concat_axis=0, tiled=True).reshape(
        tok_rows, control.shape[1]
    )
    placed = make_hint(arrived, hint_weight)
    return (attended.astype(jnp.float32) + placed.astype(jnp.float32) * gain_row).astype(
        jnp.bfloat16
    )


def row_scale(values):
    return lax.rsqrt(jnp.mean(values * values, axis=-1, keepdims=True) + 1e-06)


def kernel(
    blks,
    owners,
    query_hbm,
    key_hbm,
    value_hbm,
    query_gain_hbm,
    key_gain_hbm,
    control_hbm,
    weight_hbm,
    gain_hbm,
    owner_hbm,
    layer_smem,
    out_ref,
    query_in,
    key_in,
    value_in,
    query_gain,
    key_gain,
    control_in,
    weight,
    gains,
    owner_smem,
    stage,
    landed,
    slabs_out,
    slabs_in,
    mixed_out,
    attended,
    hint,
    load_sem,
    send_sem,
    recv_sem,
    slab_send,
    slab_recv,
    back_send,
    back_recv,
    level_sem,
):
    rows = query_in.shape[0]
    low, high = host_range(owners)
    wide = high - low
    heads = blks * wide
    cols = blks // CORES
    devices = blks * owners
    slab_rows = rows // owners
    b = lax.axis_index("blk")
    u = lax.axis_index("ulysses")
    parity = lax.rem(b, CORES)
    x = b // CORES
    me = b * owners + u
    own = b * wide + lax.rem(u - low + wide * owners, wide)
    hosting = (u >= low) & (u < high)

    loads = [
        pltpu.make_async_copy(source, target, load_sem.at[at])
        for at, (source, target) in enumerate(
            (
                (query_hbm, query_in),
                (query_gain_hbm, query_gain),
                (key_hbm, key_in),
                (key_gain_hbm, key_gain),
                (value_hbm, value_in),
                (control_hbm, control_in),
                (weight_hbm, weight),
                (gain_hbm, gains),
                (owner_hbm, owner_smem),
            )
        )
    ]
    for load in loads:
        load.start()

    around = (
        (b >= 0, {"blk": x * CORES + (1 - parity)}),
        (u > 0, {"ulysses": u - 1}),
        (u < owners - 1, {"ulysses": u + 1}),
        (x > 0, {"blk": b - CORES}),
        (x < cols - 1, {"blk": b + CORES}),
    )
    near = (
        1
        + (u + owners - 1) // owners
        + (2 * owners - 2 - u) // owners
        + (x + cols - 1) // cols
        + (2 * cols - 2 - x) // cols
    )

    def tell(semaphore):
        for inside, device in around:

            @pl.when(inside)
            def _():
                pl.semaphore_signal(
                    semaphore, inc=1, device_id=device, device_id_type=MESH
                )

    def hops(to_b, to_u):
        return (
            jnp.abs(to_b // CORES - x) + jnp.abs(lax.rem(jnp.int32(to_b), CORES) - parity) + jnp.abs(to_u - u)
        )

    reach = max(max(high - 1, owners - 1 - low) + cols, owners - 1)
    barrier = pltpu.get_barrier_semaphore()
    tell(barrier)
    pl.semaphore_wait(barrier, near)
    tell(level_sem.at[2])

    for first, gain, part in ((query_in, query_gain, 0), (key_in, key_gain, 1)):
        loads[2 * part].wait()
        loads[2 * part + 1].wait()
        values = first[...].astype(jnp.float32)
        normed = (values * row_scale(values) * gain[...]).astype(jnp.bfloat16)
        for h in range(heads):
            stage[h, part * rows : (part + 1) * rows] = normed[
                :, h * HEAD_DIM : (h + 1) * HEAD_DIM
            ]
    loads[4].wait()
    for h in range(heads):
        stage[h, 2 * rows :] = value_in[:, h * HEAD_DIM : (h + 1) * HEAD_DIM]

    started = []

    def remote(source, target, sem_out, sem_in, device):
        return pltpu.make_async_remote_copy(
            src_ref=source,
            dst_ref=target,
            send_sem=sem_out,
            recv_sem=sem_in,
            device_id=device,
            device_id_type=MESH,
        )

    def send(*way):
        copy = remote(*way)
        copy.start()
        started.append(copy)

    def arrive(target, sem_out, sem_in):
        pltpu.make_async_remote_copy(
            src_ref=target,
            dst_ref=target,
            send_sem=sem_out,
            recv_sem=sem_in,
            device_id={"blk": x * CORES + (1 - parity)},
            device_id_type=MESH,
        ).wait_recv()

    hosts = [(h, h // wide, low + h % wide) for h in range(heads)]
    for distance in range(1, reach + 1):
        if distance > 1:
            pl.semaphore_wait(level_sem.at[distance], near)
            if distance < reach:
                tell(level_sem.at[distance + 1])
        for _, base_b, to_u in hosts:
            to_b = lax.rem(b + base_b, blks)
            h = to_b * wide + to_u - low

            @pl.when(hops(to_b, to_u) == distance)
            def _():
                remote(
                    stage.at[h],
                    landed.at[me],
                    send_sem.at[h],
                    recv_sem.at[me],
                    {"blk": to_b, "ulysses": to_u},
                ).start()

    loads[5].wait()
    loads[8].wait()
    values = control_in[...].astype(jnp.float32)
    normed = values * row_scale(values)
    pieces = [normed[j * slab_rows : (j + 1) * slab_rows] for j in range(owners)]
    for to in range(owners):
        picked = pieces[0]
        for j in range(1, owners):
            picked = jnp.where(owner_smem[0, j] == to, pieces[j], picked)
        slabs_out[to] = picked.astype(jnp.bfloat16)

    for d in range(1, owners):
        there = lax.rem(u + d, owners)
        send(
            slabs_out.at[there],
            slabs_in.at[u],
            slab_send.at[d],
            slab_recv.at[u],
            {"ulysses": there},
        )
    slabs_in[u] = slabs_out[u]

    order = [
        (to_b, to_u)
        for to_u in sorted(range(owners), key=lambda at: (low <= at < high, at))
        for to_b in range(blks)
    ]
    factor = HEAD_DIM ** (-0.5) * math.log2(math.e)

    @pl.when(hosting)
    def _():
        landed[me] = stage[own]
        for to_b, to_u in order:
            there = to_b * owners + to_u

            @pl.when(there != me)
            def _():
                arrive(landed.at[there], back_send.at[0], recv_sem.at[there])

        count = devices * rows
        keys = landed[:, rows : 2 * rows].reshape(count, HEAD_DIM)
        mix = landed[:, 2 * rows :].reshape(count, HEAD_DIM)
        group = devices // GROUPS

        def flush(base):
            for to_b, to_u in order[base : base + group]:
                there = to_b * owners + to_u

                @pl.when(there != me)
                def _():
                    remote(
                        mixed_out.at[there],
                        attended.at[own],
                        back_send.at[there],
                        back_recv.at[own],
                        {"blk": to_b, "ulysses": to_u},
                    ).start()

        for base in range(0, devices, group):
            part = [to_b * owners + to_u for to_b, to_u in order[base : base + group]]
            queries = jnp.concatenate([landed[there, :rows] for there in part], axis=0)
            scores = lax.dot_general(
                queries, keys, (((1,), (1,)), ((), ())), preferred_element_type=jnp.float32
            )
            peak = jnp.max(scores, axis=-1, keepdims=True)
            expo = jnp.exp2((scores - peak) * factor)
            totals = jnp.sum(expo, axis=-1, keepdims=True)
            output = jnp.dot(
                expo.astype(jnp.bfloat16), mix, preferred_element_type=jnp.float32
            )
            output = (output * (1.0 / totals)).astype(jnp.bfloat16)
            if base:
                flush(base - group)
            for at, there in enumerate(part):
                mixed_out[there] = output[at * rows : (at + 1) * rows]
        flush(devices - group)
        attended[own] = mixed_out[me]

    loads[6].wait()
    loads[7].wait()
    for d in range(1, owners):
        source = lax.rem(u + owners - d, owners)
        arrive(slabs_in.at[source], slab_send.at[0], slab_recv.at[source])
    arrived = slabs_in[...].astype(jnp.float32).reshape(rows, control_in.shape[1])
    placed = jnp.dot(
        arrived.astype(jnp.bfloat16), weight[...], preferred_element_type=jnp.float32
    ).astype(jnp.bfloat16)
    hint[...] = placed.astype(jnp.float32) * gains[pl.ds(layer_smem[0], 1), :]

    for h, to_b, to_u in hosts:

        @pl.when(hops(to_b, to_u) > 0)
        def _():
            arrive(attended.at[h], back_send.at[0], back_recv.at[h])
            remote(
                stage.at[h], landed.at[me], send_sem.at[h], recv_sem.at[me], around[0][1]
            ).wait_send()

    for h in range(heads):
        columns = slice(h * HEAD_DIM, (h + 1) * HEAD_DIM)
        out_ref[:, columns] = (attended[h].astype(jnp.float32) + hint[:, columns]).astype(
            jnp.bfloat16
        )
    for copy in started:
        copy.wait_send()

    @pl.when(hosting)
    def _():
        for there in range(devices):

            @pl.when(there != me)
            def _():
                remote(
                    mixed_out.at[there],
                    attended.at[own],
                    back_send.at[there],
                    back_recv.at[own],
                    around[0][1],
                ).wait_send()


GROUPS = 8


def host_range(owners):
    low = owners // 4
    return (low, owners - low)


def run(blks, owners, *arrays):
    query_proj, control, hint_weight, hint_gain = arrays[0], arrays[5], arrays[6], arrays[7]
    rows, feats = query_proj.shape
    low, high = host_range(owners)
    heads = blks * (high - low)
    devices = blks * owners
    fits = (
        blks % CORES == 0
        and owners > 1
        and heads * HEAD_DIM == feats
        and devices % GROUPS == 0
        and rows % 16 == 0
        and rows % owners == 0
        and (rows // owners) % 8 == 0
        and rows * devices <= 1024
    )
    if not fits:
        return shards(*arrays)
    inner = control.shape[1]
    dma = pltpu.SemaphoreType.DMA
    half = jnp.bfloat16
    wide = jnp.float32
    operands = list(arrays)
    operands[3] = arrays[3].reshape(1, feats)
    operands[4] = arrays[4].reshape(1, feats)
    layer = operands.pop()
    operands = [pltpu.with_memory_space_constraint(array, pltpu.HBM) for array in operands]
    return pl.pallas_call(
        functools.partial(kernel, blks, owners),
        out_shape=jax.ShapeDtypeStruct((rows, feats), half),
        in_specs=[pl.BlockSpec(memory_space=pltpu.HBM)] * len(operands)
        + [pl.BlockSpec(memory_space=pltpu.SMEM)],
        out_specs=pl.BlockSpec(memory_space=pltpu.VMEM),
        scratch_shapes=[
            pltpu.VMEM((rows, feats), half),
            pltpu.VMEM((rows, feats), half),
            pltpu.VMEM((rows, feats), half),
            pltpu.VMEM((1, feats), wide),
            pltpu.VMEM((1, feats), wide),
            pltpu.VMEM((rows, inner), half),
            pltpu.VMEM(hint_weight.shape, half),
            pltpu.VMEM(hint_gain.shape, wide),
            pltpu.SMEM((1, owners), jnp.int32),
            pltpu.VMEM((heads, 3 * rows, HEAD_DIM), half),
            pltpu.VMEM((devices, 3 * rows, HEAD_DIM), half),
            pltpu.VMEM((owners, rows // owners, inner), half),
            pltpu.VMEM((owners, rows // owners, inner), half),
            pltpu.VMEM((devices, rows, HEAD_DIM), half),
            pltpu.VMEM((heads, rows, HEAD_DIM), half),
            pltpu.VMEM((rows, feats), wide),
            dma((len(operands),)),
            dma((heads,)),
            dma((devices,)),
            dma((owners,)),
            dma((owners,)),
            dma((devices,)),
            dma((heads,)),
            pltpu.SemaphoreType.REGULAR((blks // CORES + owners + 1,)),
        ],
        compiler_params=pltpu.CompilerParams(
            collective_id=0, has_side_effects=True, vmem_limit_bytes=16 << 20
        ),
    )(*operands, layer)


def solution(mesh):
    return jax.shard_map(
        functools.partial(run, mesh.shape["blk"], mesh.shape["ulysses"]),
        mesh=mesh,
        in_specs=(
            P(("groups", "blk", "ulysses"), None),
            P(("groups", "blk", "ulysses"), None),
            P(("groups", "blk", "ulysses"), None),
            P(),
            P(),
            P(("groups", "blk", "ulysses"), None),
            P(),
            P(),
            P(("groups", "blk", "ulysses"), None),
            P(("groups", "blk", "ulysses")),
        ),
        out_specs=P(("groups", "blk", "ulysses"), None),
        check_vma=False,
    )
```
